32 devices in a mesh: req: 8 (over z, x), kv: 4 (over y, core).
Axes of the slice: x: 2, y: 2, z: 4, core: 2. Of those that a mesh axis runs over, the one named last changes fastest.
Arguments:
- activations: bfloat16 [1024, 8192], P('kv', 'req'), may hold values from -210 to 210
- input_gain: bfloat16 [8192], P('req'), may hold values from 0.25 to 1.75
- qkv_weight: bfloat16 [8192, 8, 1280], P('req', 'kv'), may hold values from -0.0625 to 0.0625
- out_weight: bfloat16 [8, 1024, 8192], P('kv', None, 'req'), may hold values from -0.1875 to 0.1875
- post_gain: bfloat16 [8192], P('req'), may hold values from 0.25 to 1.75
- cache_entries: bfloat16 [40, 4096, 8, 256], P('req', None, 'kv'), may hold values from -140 to 140
- new_lengths: int32 [8, 5], replicated, may hold values from 1 to 96, 128 in all within a row
- cache_lengths: int32 [8, 5], replicated, may hold values from 1 to 4096, as said below
- request_slot: int32 [40], replicated, may hold values from 0 to 39, each once
Outputs:
- projected: bfloat16 [1024, 8192], P('kv', 'req')
- normed: bfloat16 [1024, 8192], P('kv', 'req')
- appended: bfloat16 [1024, 8, 256], P('req', 'kv')
The draws below stay inside these ranges and needn't reach their ends.
Inputs may be any that keep to these rules, and one draw needn't show every extreme that they name: `new_lengths`: the 5 requests of one block bring 128 new tokens together; in every block one request brings exactly 96. `cache_lengths`: A request's cache holds fewer than 256 positions or exactly 4096; some request holds 4096. Each number once; request q of the arrival order sits in block request_slot[q] // 5, slot request_slot[q] % 5.
All inputs are finite; a program needn't handle non-finite values.
Results may differ from the reference program's by a relative error of at most 0.012.
The reference program's roundings to bfloat16 on the way count: a program that leaves them out, or rounds other values in their place, can miss the bound.
Values may be sent and summed in bfloat16 or wider, within the bound.
A program may use at most 512 MiB of HBM per device.

```python
import math
import jax
import jax.numpy as jnp
import numpy as np
from jax import lax

D = 8192
HQ = 64
KVH = 8
HD = 128
GROUP = 8
REQ_BLK = 5
TOK_BLK = 128
MOST_NEW = 96
SLOT = 4096
SHORT = 256
TOKENS = 1024
REQS = 40
N_REQ = 8


def draw_activations(key, part):
    first_key, second_key, third_key = jax.random.split(key, 3)
    columns = jnp.arange(D, dtype=jnp.float32) / D
    rising = math.log(3.0)
    values = jnp.clip(jax.random.normal(first_key, (TOKENS, D), jnp.float32), -5.0, 5.0)
    column_scale = jnp.exp(rising * columns + jax.random.uniform(second_key, (D,), jnp.float32, -1.0, 1.0))
    row_scale = jnp.exp(jax.random.uniform(third_key, (TOKENS, 1), jnp.float32, 0.0, math.log(10.0)))
    return (values * column_scale[None, :] * row_scale * 0.5).astype(jnp.bfloat16)


def draw_cache_entries(key, part):
    first_key, second_key = jax.random.split(key, 2)
    grid_shape = (REQS, SLOT, KVH, HD)
    stored_keys = 2.0 * jnp.clip(jax.random.normal(first_key, grid_shape, jnp.float32), -5.0, 5.0)
    stored_values = jnp.clip(jax.random.normal(second_key, grid_shape, jnp.float32), -5.0, 5.0)
    return jnp.concatenate([stored_keys, stored_values], axis=-1).astype(jnp.bfloat16)


def draw_cache_lengths(key, part):
    first_key, second_key, third_key = jax.random.split(key, 3)
    grid_shape = (N_REQ, REQ_BLK)
    short_len = jax.random.randint(first_key, grid_shape, 1, SHORT)
    longer = jax.random.randint(second_key, grid_shape, 0, 8) == 0
    chosen = jax.random.randint(third_key, (), 0, N_REQ * REQ_BLK)
    flat_pick = jnp.arange(N_REQ * REQ_BLK, dtype=jnp.int32).reshape(grid_shape) == chosen
    return jnp.where(longer | flat_pick, SLOT, short_len).astype(jnp.int32)


def block_scale(stream_key, shape, cuts, low, largest):
    gain = 1.0
    for dim, parts in cuts:
        draws = jax.random.uniform(jax.random.fold_in(jax.random.fold_in(stream_key, 6), dim), (parts,), jnp.float32, low / len(cuts), largest / len(cuts))
        gain = gain * jnp.repeat(jnp.exp(draws), shape[dim] // parts).reshape((-1,) + (1,) * (len(shape) - 1 - dim))
    return gain


def profile(amount, total, reach, skew):
    weights = [(1 << 20) // math.isqrt(standing ** skew) + 1 for standing in range(2, amount + 1)]
    surplus, given = total - reach - (amount - 1), [1] * (amount - 1)
    while surplus > 0:
        candidates = [i for i in range(amount - 1) if given[i] < reach]
        whole, left = sum([weights[i] for i in candidates]), surplus
        for i in candidates:
            more = min(reach - given[i], max(1, left * weights[i] // whole), surplus)
            given[i] = given[i] + more
            surplus = surplus - more
    return np.array([reach] + given)


def uneven_parts(key, amount, total, most, lean):
    if amount == 2:
        one = jax.random.randint(key, (), max(1, total - most), min(most, total - 1) + 1)
        return jnp.stack([one, total - one])
    lengths = jnp.asarray(profile(amount, total, most, lean), jnp.int32)
    couples = (amount - 1) // 2
    source_of, sink = lengths[1:1 + 2 * couples:2], lengths[2:2 + 2 * couples:2]
    slack = jnp.minimum(source_of - 1, most - sink)
    passed = jax.random.randint(jax.random.fold_in(key, 1), (couples,), 0, 1 << 20) % (slack + 1)
    lengths = lengths.at[1:1 + 2 * couples:2].set(source_of - passed).at[2:2 + 2 * couples:2].set(sink + passed)
    return lengths[jax.random.permutation(jax.random.fold_in(key, 2), amount)]


def normal_values(own_key, dims, scale, bound, cuts=(), held_as=jnp.bfloat16):
    factor_of = block_scale(own_key, dims, cuts, -0.22, 0.18) if cuts else 1.0
    drawn = jax.random.normal(own_key, dims, jnp.float32) * scale * factor_of
    return jnp.minimum(jnp.maximum(drawn, -bound), bound).astype(held_as)


def setup_inputs(seed: int = 0) -> dict:
    seeds = jax.random.split(jax.random.key(seed), 10)
    return {
        "activations": draw_activations(jax.random.fold_in(seeds[9], 71), 0),
        "input_gain": jnp.clip(1.0 + 0.15 * jax.random.normal(seeds[1], (D,), jnp.float32), 0.25, 1.75).astype(jnp.bfloat16),
        "qkv_weight": normal_values(seeds[2], (D, KVH, (GROUP + 2) * HD), D ** -0.5, 0.0625, ((0, 8), (1, 4))),
        "out_weight": normal_values(seeds[3], (KVH, GROUP * HD, D), (GROUP * HD) ** -0.5, 0.1875, ((0, 4), (2, 8))),
        "post_gain": jnp.clip(1.0 + 0.15 * jax.random.normal(seeds[4], (D,), jnp.float32), 0.25, 1.75).astype(jnp.bfloat16),
        "cache_entries": draw_cache_entries(jax.random.fold_in(seeds[9], 71), 0),
        "new_lengths": jax.vmap(lambda own: uneven_parts(own, REQ_BLK, TOK_BLK, MOST_NEW, 2))(jax.random.split(seeds[6], N_REQ)).reshape((N_REQ, REQ_BLK)).astype(jnp.int32),
        "cache_lengths": draw_cache_lengths(jax.random.fold_in(seeds[9], 71), 0),
        "request_slot": jax.random.permutation(seeds[8], REQS).astype(jnp.int32),
    }


epsilon_norm = 1e-05
rope_base = 500000.0

def layout(new_lengths, cache_lengths, request_slot, block_tokens):
    blocks, per_block = new_lengths.shape
    request_total = blocks * per_block
    token_total = blocks * block_tokens
    slot_ids = jnp.arange(request_total, dtype=jnp.int32)
    new_flat = new_lengths.reshape(request_total).astype(jnp.int32)
    cache_flat = cache_lengths.reshape(request_total).astype(jnp.int32)
    chosen = (request_slot[:, None] == slot_ids[None, :]).astype(jnp.int32)
    arrival_len = lax.optimization_barrier(jnp.sum(chosen * new_flat[None, :], axis=1)).astype(jnp.int32)
    arrival_start = (jnp.cumsum(arrival_len) - arrival_len).astype(jnp.int32)
    inside = (jnp.cumsum(new_lengths, axis=1) - new_lengths).astype(jnp.int32)
    slot_start = (inside + block_tokens * jnp.arange(blocks, dtype=jnp.int32)[:, None]).reshape(request_total).astype(jnp.int32)
    slot_arrival_start = lax.optimization_barrier(jnp.sum(chosen * arrival_start[:, None], axis=0)).astype(jnp.int32)
    positions = jnp.arange(token_total, dtype=jnp.int32)
    slot_of_row = (lax.optimization_barrier(jnp.sum((slot_start[None, :] <= positions[:, None]).astype(jnp.int32), axis=1)) - 1).astype(jnp.int32)
    row_pick = (slot_of_row[:, None] == slot_ids[None, :]).astype(jnp.int32)
    offset_row = (positions - lax.optimization_barrier(jnp.sum(row_pick * slot_start[None, :], axis=1))).astype(jnp.int32)
    token_of_row = (lax.optimization_barrier(jnp.sum(row_pick * slot_arrival_start[None, :], axis=1)) + offset_row).astype(jnp.int32)
    pos_of_row = (lax.optimization_barrier(jnp.sum(row_pick * cache_flat[None, :], axis=1)) + offset_row).astype(jnp.int32)
    arrival_of_token = (lax.optimization_barrier(jnp.sum((arrival_start[None, :] <= positions[:, None]).astype(jnp.int32), axis=1)) - 1).astype(jnp.int32)
    token_pick = (arrival_of_token[:, None] == slot_ids[None, :]).astype(jnp.int32)
    slot_of_token = lax.optimization_barrier(jnp.sum(token_pick * request_slot[None, :], axis=1)).astype(jnp.int32)
    offset_token = (positions - lax.optimization_barrier(jnp.sum(token_pick * arrival_start[None, :], axis=1))).astype(jnp.int32)
    token_slot_pick = (slot_of_token[:, None] == slot_ids[None, :]).astype(jnp.int32)
    row_of_token = (lax.optimization_barrier(jnp.sum(token_slot_pick * slot_start[None, :], axis=1)) + offset_token).astype(jnp.int32)
    pos_of_token = (lax.optimization_barrier(jnp.sum(token_slot_pick * cache_flat[None, :], axis=1)) + offset_token).astype(jnp.int32)
    return (token_of_row, row_of_token, pos_of_row, pos_of_token, slot_of_row, offset_row, slot_start)

def rotate(partial_sums, positions, group_size, head_size):
    half_size = head_size // 2
    frequency = jnp.exp(-(jnp.arange(half_size, dtype=jnp.float32) * (2.0 / head_size)) * math.log(rope_base))
    angles = positions.astype(jnp.float32)[:, None] * frequency[None, :]
    cosine = jnp.cos(angles)[:, None, None, :]
    sine_part = jnp.sin(angles)[:, None, None, :]
    turned = partial_sums[:, :, :group_size + 1, :]
    first_half = turned[..., :half_size]
    second_half = turned[..., half_size:]
    turned = jnp.concatenate([first_half * cosine - second_half * sine_part, second_half * cosine + first_half * sine_part], axis=-1)
    return jnp.concatenate([turned, partial_sums[:, :, group_size + 1:, :]], axis=2)

def reference(activations, input_gain, qkv_weight, out_weight, post_gain, cache_entries, new_lengths, cache_lengths, request_slot):
    group_size = HQ // KVH
    inputs_f32 = activations.astype(jnp.float32)
    normed_in = (inputs_f32 * lax.rsqrt(lax.optimization_barrier(jnp.mean(inputs_f32 * inputs_f32, axis=1, keepdims=True)) + epsilon_norm) * input_gain.astype(jnp.float32)[None, :]).astype(jnp.bfloat16)
    token_of_row, row_of_token, pos_of_row, pos_of_token, slot_of_row, offset_row, slot_start = layout(new_lengths, cache_lengths, request_slot, TOK_BLK)
    qkv_sums = jnp.dot(normed_in, qkv_weight.reshape(D, KVH * (group_size + 2) * HD), preferred_element_type=jnp.float32)
    rotated = rotate(qkv_sums.reshape(TOKENS, KVH, group_size + 2, HD), pos_of_token, group_size, HD).astype(jnp.bfloat16)
    block_rows = jnp.take(rotated, token_of_row, axis=0)
    appended = block_rows[:, :, group_size:, :].reshape(TOKENS, KVH, 2 * HD)
    new_flat = new_lengths.reshape(REQS).astype(jnp.int32)
    cache_flat = cache_lengths.reshape(REQS).astype(jnp.int32)
    score_scale = 1.0 / math.sqrt(HD)

    def one_slot(slot_index):
        block_index = slot_index // REQ_BLK
        offsets = jnp.arange(MOST_NEW, dtype=jnp.int32)
        picked = jnp.minimum(slot_start[slot_index] + offsets, block_index * TOK_BLK + TOK_BLK - 1).astype(jnp.int32)
        slot_rows = jnp.take(block_rows, picked, axis=0).astype(jnp.float32)
        queries = slot_rows[:, :, :group_size, :]
        new_keys = slot_rows[:, :, group_size, :]
        new_values = slot_rows[:, :, group_size + 1, :]
        stored = lax.dynamic_index_in_dim(cache_entries, slot_index, 0, keepdims=False).astype(jnp.float32)
        cached_count = cache_flat[slot_index]
        new_count = new_flat[slot_index]
        cache_scores = jnp.einsum('ihgd,khd->hgik', queries, stored[..., :HD]) * score_scale
        cache_valid = jnp.arange(SLOT, dtype=jnp.int32) < cached_count
        cache_scores = jnp.where(cache_valid[None, None, None, :], cache_scores, -jnp.inf)
        new_valid = (offsets[None, :] <= offsets[:, None]) & (offsets[None, :] < new_count)
        new_scores = jnp.einsum('ihgd,jhd->hgij', queries, new_keys) * score_scale
        new_scores = jnp.where(new_valid[None, None], new_scores, -jnp.inf)
        highest = jnp.maximum(lax.optimization_barrier(jnp.max(cache_scores, axis=-1)), lax.optimization_barrier(jnp.max(new_scores, axis=-1)))
        cache_weights = jnp.exp(cache_scores - highest[..., None])
        new_weights = jnp.exp(new_scores - highest[..., None])
        totals = lax.optimization_barrier(jnp.sum(cache_weights, axis=-1)) + lax.optimization_barrier(jnp.sum(new_weights, axis=-1))
        cache_rounded = lax.optimization_barrier(cache_weights.astype(jnp.bfloat16)).astype(jnp.float32)
        new_rounded = lax.optimization_barrier(new_weights.astype(jnp.bfloat16)).astype(jnp.float32)
        summed = jnp.einsum('hgik,khd->ihgd', cache_rounded, stored[..., HD:]) + jnp.einsum('hgij,jhd->ihgd', new_rounded, new_values)
        return (summed / jnp.transpose(totals, (2, 0, 1))[..., None]).astype(jnp.bfloat16)
    stacked = lax.map(one_slot, jnp.arange(REQS, dtype=jnp.int32))
    flat_rows = stacked.reshape(REQS * MOST_NEW, KVH * group_size * HD)
    attention = jnp.take(flat_rows, (slot_of_row * MOST_NEW + offset_row).astype(jnp.int32), axis=0)
    token_attention = jnp.take(attention, row_of_token, axis=0)
    projection = jnp.dot(token_attention, out_weight.reshape(KVH * group_size * HD, D), preferred_element_type=jnp.float32)
    projected = projection.astype(jnp.bfloat16)
    residual = inputs_f32 + projection
    normed = (residual * lax.rsqrt(lax.optimization_barrier(jnp.mean(residual * residual, axis=1, keepdims=True)) + epsilon_norm) * post_gain.astype(jnp.float32)[None, :]).astype(jnp.bfloat16)
    return (projected, normed, appended)
```

```python
import functools
import math

import jax
import jax.numpy as jnp
from jax import lax
from jax.experimental import pallas as pl
from jax.experimental.pallas import tpu as pltpu
from jax.sharding import PartitionSpec as P

epsilon_norm = 1e-05
rope_base = 500000.0


def layout(new_lengths, cache_lengths, request_slot, block_tokens):
    blocks, per_block = new_lengths.shape
    request_total = blocks * per_block
    token_total = blocks * block_tokens
    slot_ids = jnp.arange(request_total, dtype=jnp.int32)
    new_flat = new_lengths.reshape(request_total)
    cache_flat = cache_lengths.reshape(request_total)
    chosen = (request_slot[:, None] == slot_ids[None, :]).astype(jnp.int32)
    arrival_len = jnp.sum(chosen * new_flat[None, :], axis=1)
    arrival_start = jnp.cumsum(arrival_len) - arrival_len
    inside = jnp.cumsum(new_lengths, axis=1) - new_lengths
    slot_start = (inside + block_tokens * jnp.arange(blocks, dtype=jnp.int32)[:, None]).reshape(
        request_total
    )
    slot_arrival_start = jnp.sum(chosen * arrival_start[:, None], axis=0)
    positions = jnp.arange(token_total, dtype=jnp.int32)
    slot_of_row = jnp.sum((slot_start[None, :] <= positions[:, None]).astype(jnp.int32), axis=1) - 1
    row_pick = (slot_of_row[:, None] == slot_ids[None, :]).astype(jnp.int32)
    offset_row = positions - jnp.sum(row_pick * slot_start[None, :], axis=1)
    token_of_row = jnp.sum(row_pick * slot_arrival_start[None, :], axis=1) + offset_row
    pos_of_row = jnp.sum(row_pick * cache_flat[None, :], axis=1) + offset_row
    arrival_of_token = (
        jnp.sum((arrival_start[None, :] <= positions[:, None]).astype(jnp.int32), axis=1) - 1
    )
    token_pick = (arrival_of_token[:, None] == slot_ids[None, :]).astype(jnp.int32)
    slot_of_token = jnp.sum(token_pick * request_slot[None, :], axis=1)
    offset_token = positions - jnp.sum(token_pick * arrival_start[None, :], axis=1)
    token_slot_pick = (slot_of_token[:, None] == slot_ids[None, :]).astype(jnp.int32)
    row_of_token = jnp.sum(token_slot_pick * slot_start[None, :], axis=1) + offset_token
    pos_of_token = jnp.sum(token_slot_pick * cache_flat[None, :], axis=1) + offset_token
    return (token_of_row, row_of_token, pos_of_row, pos_of_token, slot_of_row, offset_row)


def rotate(partial_sums, positions, group_size, head_size):
    half_size = head_size // 2
    frequency = jnp.exp(
        -(jnp.arange(half_size, dtype=jnp.float32) * (2.0 / head_size)) * math.log(rope_base)
    )
    angles = positions.astype(jnp.float32)[:, None] * frequency[None, :]
    cosine = jnp.cos(angles)[:, None, None, :]
    sine_part = jnp.sin(angles)[:, None, None, :]
    turned = partial_sums[:, :, : group_size + 1, :]
    first_half = turned[..., :half_size]
    second_half = turned[..., half_size:]
    turned = jnp.concatenate(
        [
            first_half * cosine - second_half * sine_part,
            second_half * cosine + first_half * sine_part,
        ],
        axis=-1,
    )
    return jnp.concatenate([turned, partial_sums[:, :, group_size + 1 :, :]], axis=2)


def attention_kernel(
    group_size, key_block, cached_ref, new_ref, q_ref, key_ref, value_ref, stored_ref, out_ref, keys, values, scores
):
    slot = pl.program_id(0)
    cached_count = cached_ref[slot]
    new_count = new_ref[slot]
    heads, rows_all, head_size = q_ref.shape[1:]
    most_new = key_ref.shape[2]
    slot_length = stored_ref.shape[1]
    chunk = min(256, rows_all)
    chunk_tokens = chunk // group_size
    block_count = (cached_count + key_block - 1) // key_block
    scale = math.log2(math.e) / math.sqrt(head_size)

    def split_heads(index, carry):
        at = pl.ds(pl.multiple_of(index * key_block, key_block), key_block)
        for head in range(heads):
            piece = stored_ref[0, at, head, :]
            keys[head, at, :] = piece[:, :head_size]
            values[head, at, :] = piece[:, head_size:]
        return carry

    lax.fori_loop(0, block_count, split_heads, 0)

    def lane_fold(op, value):
        folded = value[:, :head_size]
        for part in range(1, value.shape[1] // head_size):
            folded = op(folded, value[:, part * head_size : (part + 1) * head_size])
        return folded

    contract_last = (((1,), (1,)), ((), ()))
    for head in range(heads):
        for part in range(rows_all // chunk):

            @pl.when(part * chunk_tokens < new_count)
            def _(head=head, part=part):
                rows = pl.ds(part * chunk, chunk)
                query = q_ref[0, head, rows, :]
                columns = lax.broadcasted_iota(jnp.int32, (chunk, most_new), 1)
                offsets = part * chunk_tokens + (
                    lax.broadcasted_iota(jnp.int32, (chunk, most_new), 0) // group_size
                )
                own = lax.dot_general(
                    query, key_ref[0, head], contract_last, preferred_element_type=jnp.float32
                )
                own = jnp.where((columns <= offsets) & (columns < new_count), own, -jnp.inf)
                places = lax.broadcasted_iota(jnp.int32, (chunk, key_block), 1)

                def fill(index, highest):
                    first = pl.multiple_of(index * key_block, key_block)
                    found = lax.dot_general(
                        query,
                        keys[head, pl.ds(first, key_block), :],
                        contract_last,
                        preferred_element_type=jnp.float32,
                    )
                    found = jnp.where(places < cached_count - first, found, -jnp.inf)
                    scores[:, pl.ds(first, key_block)] = found
                    return jnp.maximum(highest, lane_fold(jnp.maximum, found))

                highest = lax.fori_loop(
                    0, block_count, fill, jnp.full((chunk, head_size), -jnp.inf, jnp.float32)
                )
                top = jnp.maximum(
                    jnp.max(highest, axis=1, keepdims=True), jnp.max(own, axis=1, keepdims=True)
                )
                own_weights = jnp.exp2((own - top) * scale)
                summed = jnp.dot(
                    own_weights.astype(jnp.bfloat16),
                    value_ref[0, head],
                    preferred_element_type=jnp.float32,
                )

                def accumulate(index, pair):
                    first = pl.multiple_of(index * key_block, key_block)
                    weights = jnp.exp2((scores[:, pl.ds(first, key_block)] - top) * scale)
                    added = jnp.dot(
                        weights.astype(jnp.bfloat16),
                        values[head, pl.ds(first, key_block), :],
                        preferred_element_type=jnp.float32,
                    )
                    return (pair[0] + lane_fold(jnp.add, weights), pair[1] + added)

                totals, summed = lax.fori_loop(
                    0,
                    block_count,
                    accumulate,
                    (jnp.zeros((chunk, head_size), jnp.float32), summed),
                )
                total = jnp.sum(totals, axis=1, keepdims=True) + jnp.sum(
                    own_weights, axis=1, keepdims=True
                )
                out_ref[0, head, rows, :] = (summed / total).astype(out_ref.dtype)


def block_attention(queries, new_keys, new_values, stored, cached_counts, new_counts, group_size):
    slots, heads, rows, head_size = queries.shape
    most_new = new_keys.shape[2]
    slot_length = stored.shape[1]
    key_block = min(512, slot_length)
    grid_spec = pltpu.PrefetchScalarGridSpec(
        num_scalar_prefetch=2,
        grid=(slots,),
        in_specs=[
            pl.BlockSpec((1, heads, rows, head_size), lambda s, c, n: (s, 0, 0, 0)),
            pl.BlockSpec((1, heads, most_new, head_size), lambda s, c, n: (s, 0, 0, 0)),
            pl.BlockSpec((1, heads, most_new, head_size), lambda s, c, n: (s, 0, 0, 0)),
            pl.BlockSpec((1, slot_length, heads, 2 * head_size), lambda s, c, n: (s, 0, 0, 0)),
        ],
        out_specs=pl.BlockSpec((1, heads, rows, head_size), lambda s, c, n: (s, 0, 0, 0)),
        scratch_shapes=[
            pltpu.VMEM((heads, slot_length, head_size), jnp.bfloat16),
            pltpu.VMEM((heads, slot_length, head_size), jnp.bfloat16),
            pltpu.VMEM((min(256, rows), slot_length), jnp.float32),
        ],
    )
    return pl.pallas_call(
        functools.partial(attention_kernel, group_size, key_block),
        grid_spec=grid_spec,
        out_shape=jax.ShapeDtypeStruct(queries.shape, jnp.bfloat16),
        compiler_params=pltpu.CompilerParams(vmem_limit_bytes=48 << 20),
    )(cached_counts, new_counts, queries, new_keys, new_values, stored)


def per_device(
    activations,
    input_gain,
    qkv_weight,
    out_weight,
    post_gain,
    cache_entries,
    new_lengths,
    cache_lengths,
    request_slot,
):
    req_count = lax.axis_size("req")
    kv_count = lax.axis_size("kv")
    token_count = activations.shape[0] * kv_count
    tok_blk = token_count // req_count
    query_rows = tok_blk * 3 // 4
    width_slice = activations.shape[1]
    width_all = width_slice * req_count
    kvh_local = qkv_weight.shape[1]
    head_size = cache_entries.shape[3] // 2
    group_size = qkv_weight.shape[2] // head_size - 2
    per_block = cache_entries.shape[0]
    token_of_row, row_of_token, pos_of_row, pos_of_token, slot_of_row, offset_row = layout(
        new_lengths, cache_lengths, request_slot, tok_blk
    )
    inputs_f32 = activations.astype(jnp.float32)
    square_total = lax.psum(jnp.sum(inputs_f32 * inputs_f32, axis=1), "req")
    normed_in = (
        inputs_f32
        * lax.rsqrt(square_total / width_all + epsilon_norm)[:, None]
        * input_gain.astype(jnp.float32)[None, :]
    ).astype(jnp.bfloat16)
    rows_all = lax.all_gather(normed_in, "kv", axis=0, tiled=True)
    rows_all = jnp.take(rows_all, token_of_row, axis=0)
    weight_flat = qkv_weight.reshape(width_slice, -1)
    block_id = lax.axis_index("req")
    first_row = block_id * tok_blk
    qkv_sums = lax.psum_scatter(
        jnp.dot(rows_all, weight_flat, preferred_element_type=jnp.float32),
        "req",
        scatter_dimension=0,
        tiled=True,
    )
    my_positions = lax.dynamic_slice_in_dim(pos_of_row, first_row, tok_blk, 0)
    rotated = rotate(
        qkv_sums.reshape(tok_blk, kvh_local, group_size + 2, head_size),
        my_positions,
        group_size,
        head_size,
    ).astype(jnp.bfloat16)
    appended = rotated[:, :, group_size:, :].reshape(tok_blk, kvh_local, 2 * head_size)
    new_counts = lax.dynamic_index_in_dim(new_lengths, block_id, 0, keepdims=False)
    cached_counts = lax.dynamic_index_in_dim(cache_lengths, block_id, 0, keepdims=False)
    starts = jnp.cumsum(new_counts) - new_counts
    picked = jnp.minimum(
        starts[:, None] + jnp.arange(query_rows, dtype=jnp.int32)[None, :], tok_blk - 1
    ).reshape(-1)
    slot_rows = jnp.take(rotated.reshape(tok_blk, -1), picked, axis=0).reshape(
        per_block, query_rows, kvh_local, group_size + 2, head_size
    )
    queries = jnp.transpose(slot_rows[:, :, :, :group_size], (0, 2, 1, 3, 4)).reshape(
        per_block, kvh_local, query_rows * group_size, head_size
    )
    stacked = block_attention(
        queries,
        jnp.transpose(slot_rows[:, :, :, group_size], (0, 2, 1, 3)),
        jnp.transpose(slot_rows[:, :, :, group_size + 1], (0, 2, 1, 3)),
        cache_entries,
        cached_counts,
        new_counts,
        group_size,
    )
    stacked = jnp.transpose(
        stacked.reshape(per_block, kvh_local, query_rows, -1), (0, 2, 1, 3)
    ).reshape(per_block * query_rows, -1)
    local_slot = lax.dynamic_slice_in_dim(slot_of_row, first_row, tok_blk, 0) - block_id * per_block
    local_offset = lax.dynamic_slice_in_dim(offset_row, first_row, tok_blk, 0)
    attention = jnp.take(stacked, local_slot * query_rows + local_offset, axis=0)
    out_flat = out_weight.reshape(-1, width_slice)
    block_projection = jnp.dot(
        lax.all_gather(attention, "req", axis=0, tiled=True),
        out_flat,
        preferred_element_type=jnp.float32,
    )
    token_rows = jnp.take(block_projection.astype(jnp.bfloat16), row_of_token, axis=0)
    projection = lax.psum_scatter(
        token_rows, "kv", scatter_dimension=0, tiled=True
    ).astype(jnp.float32)
    projected = projection.astype(jnp.bfloat16)
    residual = inputs_f32 + projection
    residual_total = lax.psum(jnp.sum(residual * residual, axis=1), "req")
    normed = (
        residual
        * lax.rsqrt(residual_total / width_all + epsilon_norm)[:, None]
        * post_gain.astype(jnp.float32)[None, :]
    ).astype(jnp.bfloat16)
    return (projected, normed, appended)


def solution(mesh):
    in_specs = (
        P("kv", "req"),
        P("req"),
        P("req", "kv", None),
        P("kv", None, "req"),
        P("req"),
        P("req", None, "kv", None),
        P(),
        P(),
        P(),
    )
    out_specs = (P("kv", "req"), P("kv", "req"), P("req", "kv", None))
    return jax.shard_map(
        per_device, mesh=mesh, in_specs=in_specs, out_specs=out_specs, check_vma=False
    )
```

```python
import functools
import math

import jax
import jax.numpy as jnp
import numpy as np
from jax import lax
from jax.experimental import pallas as pl
from jax.experimental.pallas import tpu as pltpu
from jax.sharding import PartitionSpec as P

epsilon_norm = 1e-05
rope_base = 500000.0


def layout(new_lengths, cache_lengths, request_slot, block_tokens):
    blocks, per_block = new_lengths.shape
    request_total = blocks * per_block
    token_total = blocks * block_tokens
    slot_ids = jnp.arange(request_total, dtype=jnp.int32)
    new_flat = new_lengths.reshape(request_total)
    cache_flat = cache_lengths.reshape(request_total)
    chosen = (request_slot[:, None] == slot_ids[None, :]).astype(jnp.int32)
    arrival_len = jnp.sum(chosen * new_flat[None, :], axis=1)
    arrival_start = jnp.cumsum(arrival_len) - arrival_len
    inside = jnp.cumsum(new_lengths, axis=1) - new_lengths
    slot_start = (inside + block_tokens * jnp.arange(blocks, dtype=jnp.int32)[:, None]).reshape(
        request_total
    )
    slot_arrival_start = jnp.sum(chosen * arrival_start[:, None], axis=0)
    positions = jnp.arange(token_total, dtype=jnp.int32)
    slot_of_row = jnp.sum((slot_start[None, :] <= positions[:, None]).astype(jnp.int32), axis=1) - 1
    row_pick = (slot_of_row[:, None] == slot_ids[None, :]).astype(jnp.int32)
    offset_row = positions - jnp.sum(row_pick * slot_start[None, :], axis=1)
    token_of_row = jnp.sum(row_pick * slot_arrival_start[None, :], axis=1) + offset_row
    pos_of_row = jnp.sum(row_pick * cache_flat[None, :], axis=1) + offset_row
    arrival_of_token = (
        jnp.sum((arrival_start[None, :] <= positions[:, None]).astype(jnp.int32), axis=1) - 1
    )
    token_pick = (arrival_of_token[:, None] == slot_ids[None, :]).astype(jnp.int32)
    slot_of_token = jnp.sum(token_pick * request_slot[None, :], axis=1)
    offset_token = positions - jnp.sum(token_pick * arrival_start[None, :], axis=1)
    token_slot_pick = (slot_of_token[:, None] == slot_ids[None, :]).astype(jnp.int32)
    row_of_token = jnp.sum(token_slot_pick * slot_start[None, :], axis=1) + offset_token
    pos_of_token = jnp.sum(token_slot_pick * cache_flat[None, :], axis=1) + offset_token
    return (token_of_row, row_of_token, pos_of_row, pos_of_token, slot_of_row, offset_row)


def rotate(partial_sums, positions, group_size, head_size):
    half_size = head_size // 2
    frequency = jnp.exp(
        -(jnp.arange(half_size, dtype=jnp.float32) * (2.0 / head_size)) * math.log(rope_base)
    )
    angles = positions.astype(jnp.float32)[:, None] * frequency[None, :]
    cosine = jnp.cos(angles)[:, None, None, :]
    sine_part = jnp.sin(angles)[:, None, None, :]
    turned = partial_sums[:, :, : group_size + 1, :]
    first_half = turned[..., :half_size]
    second_half = turned[..., half_size:]
    turned = jnp.concatenate(
        [
            first_half * cosine - second_half * sine_part,
            second_half * cosine + first_half * sine_part,
        ],
        axis=-1,
    )
    return jnp.concatenate([turned, partial_sums[:, :, group_size + 1 :, :]], axis=2)


def attention_kernel(
    group_size, key_block, cached_ref, new_ref, q_ref, key_ref, value_ref, stored_ref, out_ref, keys, values, scores
):
    slot = pl.program_id(0)
    cached_count = cached_ref[slot]
    new_count = new_ref[slot]
    heads, rows_all, head_size = q_ref.shape[1:]
    most_new = key_ref.shape[2]
    slot_length = stored_ref.shape[1]
    chunk = min(256, rows_all)
    chunk_tokens = chunk // group_size
    block_count = (cached_count + key_block - 1) // key_block
    scale = math.log2(math.e) / math.sqrt(head_size)

    def split_heads(index, carry):
        at = pl.ds(pl.multiple_of(index * key_block, key_block), key_block)
        for head in range(heads):
            piece = stored_ref[0, at, head, :]
            keys[head, at, :] = piece[:, :head_size]
            values[head, at, :] = piece[:, head_size:]
        return carry

    lax.fori_loop(0, block_count, split_heads, 0)

    def lane_fold(op, value):
        folded = value[:, :head_size]
        for part in range(1, value.shape[1] // head_size):
            folded = op(folded, value[:, part * head_size : (part + 1) * head_size])
        return folded

    contract_last = (((1,), (1,)), ((), ()))
    for head in range(heads):
        for part in range(rows_all // chunk):

            @pl.when(part * chunk_tokens < new_count)
            def _(head=head, part=part):
                rows = pl.ds(part * chunk, chunk)
                query = q_ref[0, head, rows, :]
                columns = lax.broadcasted_iota(jnp.int32, (chunk, most_new), 1)
                offsets = part * chunk_tokens + (
                    lax.broadcasted_iota(jnp.int32, (chunk, most_new), 0) // group_size
                )
                own = lax.dot_general(
                    query, key_ref[0, head], contract_last, preferred_element_type=jnp.float32
                )
                own = jnp.where((columns <= offsets) & (columns < new_count), own, -jnp.inf)
                places = lax.broadcasted_iota(jnp.int32, (chunk, key_block), 1)

                def fill(index, highest):
                    first = pl.multiple_of(index * key_block, key_block)
                    found = lax.dot_general(
                        query,
                        keys[head, pl.ds(first, key_block), :],
                        contract_last,
                        preferred_element_type=jnp.float32,
                    )
                    found = jnp.where(places < cached_count - first, found, -jnp.inf)
                    scores[:, pl.ds(first, key_block)] = found
                    return jnp.maximum(highest, lane_fold(jnp.maximum, found))

                highest = lax.fori_loop(
                    0, block_count, fill, jnp.full((chunk, head_size), -jnp.inf, jnp.float32)
                )
                top = jnp.maximum(
                    jnp.max(highest, axis=1, keepdims=True), jnp.max(own, axis=1, keepdims=True)
                )
                own_weights = jnp.exp2((own - top) * scale)
                summed = jnp.dot(
                    own_weights.astype(jnp.bfloat16),
                    value_ref[0, head],
                    preferred_element_type=jnp.float32,
                )

                def accumulate(index, pair):
                    first = pl.multiple_of(index * key_block, key_block)
                    weights = jnp.exp2((scores[:, pl.ds(first, key_block)] - top) * scale)
                    added = jnp.dot(
                        weights.astype(jnp.bfloat16),
                        values[head, pl.ds(first, key_block), :],
                        preferred_element_type=jnp.float32,
                    )
                    return (pair[0] + lane_fold(jnp.add, weights), pair[1] + added)

                totals, summed = lax.fori_loop(
                    0,
                    block_count,
                    accumulate,
                    (jnp.zeros((chunk, head_size), jnp.float32), summed),
                )
                total = jnp.sum(totals, axis=1, keepdims=True) + jnp.sum(
                    own_weights, axis=1, keepdims=True
                )
                out_ref[0, head, rows, :] = (summed / total).astype(out_ref.dtype)


def block_attention(queries, new_keys, new_values, stored, cached_counts, new_counts, group_size):
    slots, heads, rows, head_size = queries.shape
    most_new = new_keys.shape[2]
    slot_length = stored.shape[1]
    key_block = min(512, slot_length)
    grid_spec = pltpu.PrefetchScalarGridSpec(
        num_scalar_prefetch=2,
        grid=(slots,),
        in_specs=[
            pl.BlockSpec((1, heads, rows, head_size), lambda s, c, n: (s, 0, 0, 0)),
            pl.BlockSpec((1, heads, most_new, head_size), lambda s, c, n: (s, 0, 0, 0)),
            pl.BlockSpec((1, heads, most_new, head_size), lambda s, c, n: (s, 0, 0, 0)),
            pl.BlockSpec((1, slot_length, heads, 2 * head_size), lambda s, c, n: (s, 0, 0, 0)),
        ],
        out_specs=pl.BlockSpec((1, heads, rows, head_size), lambda s, c, n: (s, 0, 0, 0)),
        scratch_shapes=[
            pltpu.VMEM((heads, slot_length, head_size), jnp.bfloat16),
            pltpu.VMEM((heads, slot_length, head_size), jnp.bfloat16),
            pltpu.VMEM((min(256, rows), slot_length), jnp.float32),
        ],
    )
    return pl.pallas_call(
        functools.partial(attention_kernel, group_size, key_block),
        grid_spec=grid_spec,
        out_shape=jax.ShapeDtypeStruct(queries.shape, jnp.bfloat16),
        compiler_params=pltpu.CompilerParams(vmem_limit_bytes=48 << 20),
    )(cached_counts, new_counts, queries, new_keys, new_values, stored)


def ring_table(count):
    across = 1
    while 4 * across * across <= count:
        across *= 2
    along = count // across
    ring = [place * across for place in range(along)]
    for turn, place in enumerate(reversed(range(along))):
        row = [place * across + step for step in range(1, across)]
        ring += row if turn % 2 == 0 else row[::-1]
    order = np.zeros((count, count), np.int32)
    slot_of = np.zeros((count, count), np.int32)
    for start in range(count):
        for step in range(count):
            order[ring[start], step] = ring[(start + step) % count]
            slot_of[ring[start], ring[(start + step) % count]] = step
    ahead = [(ring[i], ring[(i + 1) % count]) for i in range(count)]
    return order, slot_of, ahead, [(b, a) for a, b in ahead]


def ring_project_scatter(rows, weight, count, ahead, behind):
    block = rows.shape[0] // count
    columns = weight.shape[1]
    parts = 2
    width = columns // parts
    made = {}

    def product(index):
        if index not in made:
            made[index] = jnp.dot(
                rows[index * block : (index + 1) * block],
                weight,
                preferred_element_type=jnp.float32,
            )
        return made[index]

    def piece(index, part):
        return product(index % count)[:, part * width : (part + 1) * width]

    forward = [part % 2 == 0 for part in range(parts)]
    held = [piece(-1 if forward[part] else 1, part) for part in range(parts)]
    for step in range(count - 1):
        moved = [
            lax.ppermute(held[part], "req", ahead if forward[part] else behind)
            for part in range(parts)
        ]
        held = [
            moved[part] + piece(-2 - step if forward[part] else 2 + step, part)
            for part in range(parts)
        ]
    return jnp.concatenate(held, axis=1)


def ring_gather_project(own, weight, count, ahead, behind):
    results = [None] * count
    results[0] = jnp.dot(own, weight, preferred_element_type=jnp.float32).astype(jnp.bfloat16)
    half = own.shape[1] // 2
    from_behind = from_ahead = own
    for step in range(1, (count + 1) // 2):
        from_behind = lax.ppermute(from_behind, "req", ahead)
        from_ahead = lax.ppermute(from_ahead, "req", behind)
        for index, arrived in ((count - step, from_behind), (step, from_ahead)):
            results[index] = jnp.dot(
                arrived, weight, preferred_element_type=jnp.float32
            ).astype(jnp.bfloat16)
    if count % 2 == 0:
        last = jnp.concatenate(
            [
                lax.ppermute(from_behind[:, :half], "req", ahead),
                lax.ppermute(from_ahead[:, half:], "req", behind),
            ],
            axis=1,
        )
        results[count // 2] = jnp.dot(
            last, weight, preferred_element_type=jnp.float32
        ).astype(jnp.bfloat16)
    return jnp.concatenate(results, axis=0)


def per_device(
    activations,
    input_gain,
    qkv_weight,
    out_weight,
    post_gain,
    cache_entries,
    new_lengths,
    cache_lengths,
    request_slot,
):
    req_count = lax.axis_size("req")
    kv_count = lax.axis_size("kv")
    token_count = activations.shape[0] * kv_count
    tok_blk = token_count // req_count
    query_rows = tok_blk * 3 // 4
    width_slice = activations.shape[1]
    width_all = width_slice * req_count
    kvh_local = qkv_weight.shape[1]
    head_size = cache_entries.shape[3] // 2
    group_size = qkv_weight.shape[2] // head_size - 2
    per_block = cache_entries.shape[0]
    token_of_row, row_of_token, pos_of_row, pos_of_token, slot_of_row, offset_row = layout(
        new_lengths, cache_lengths, request_slot, tok_blk
    )
    inputs_f32 = activations.astype(jnp.float32)
    square_total = lax.psum(jnp.sum(inputs_f32 * inputs_f32, axis=1), "req")
    normed_in = (
        inputs_f32
        * lax.rsqrt(square_total / width_all + epsilon_norm)[:, None]
        * input_gain.astype(jnp.float32)[None, :]
    ).astype(jnp.bfloat16)
    rows_all = lax.all_gather(normed_in, "kv", axis=0, tiled=True)
    block_id = lax.axis_index("req")
    first_row = block_id * tok_blk
    order, slot_of, ahead, behind = ring_table(req_count)
    ring_order = lax.dynamic_index_in_dim(jnp.asarray(order), block_id, 0, keepdims=False)
    ring_slot = lax.dynamic_index_in_dim(jnp.asarray(slot_of), block_id, 0, keepdims=False)
    ring_pick = (
        ring_order[:, None] == jnp.arange(req_count, dtype=jnp.int32)[None, :]
    ).astype(jnp.int32)
    ring_rows = jnp.sum(
        ring_pick[:, :, None] * token_of_row.reshape(req_count, tok_blk)[None], axis=1
    ).reshape(-1)
    rows_all = jnp.take(rows_all, ring_rows, axis=0, mode="clip")
    weight_flat = qkv_weight.reshape(width_slice, -1)
    qkv_sums = ring_project_scatter(rows_all, weight_flat, req_count, ahead, behind)
    my_positions = lax.dynamic_slice_in_dim(pos_of_row, first_row, tok_blk, 0)
    rotated = rotate(
        qkv_sums.reshape(tok_blk, kvh_local, group_size + 2, head_size),
        my_positions,
        group_size,
        head_size,
    ).astype(jnp.bfloat16)
    appended = rotated[:, :, group_size:, :].reshape(tok_blk, kvh_local, 2 * head_size)
    new_counts = lax.dynamic_index_in_dim(new_lengths, block_id, 0, keepdims=False)
    cached_counts = lax.dynamic_index_in_dim(cache_lengths, block_id, 0, keepdims=False)
    starts = jnp.cumsum(new_counts) - new_counts
    picked = jnp.minimum(
        starts[:, None] + jnp.arange(query_rows, dtype=jnp.int32)[None, :], tok_blk - 1
    ).reshape(-1)
    slot_rows = jnp.take(rotated.reshape(tok_blk, -1), picked, axis=0, mode="clip").reshape(
        per_block, query_rows, kvh_local, group_size + 2, head_size
    )
    queries = jnp.transpose(slot_rows[:, :, :, :group_size], (0, 2, 1, 3, 4)).reshape(
        per_block, kvh_local, query_rows * group_size, head_size
    )
    stacked = block_attention(
        queries,
        jnp.transpose(slot_rows[:, :, :, group_size], (0, 2, 1, 3)),
        jnp.transpose(slot_rows[:, :, :, group_size + 1], (0, 2, 1, 3)),
        cache_entries,
        cached_counts,
        new_counts,
        group_size,
    )
    stacked = jnp.transpose(
        stacked.reshape(per_block, kvh_local, query_rows, -1), (0, 2, 1, 3)
    ).reshape(per_block * query_rows, -1)
    local_slot = lax.dynamic_slice_in_dim(slot_of_row, first_row, tok_blk, 0) - block_id * per_block
    local_offset = lax.dynamic_slice_in_dim(offset_row, first_row, tok_blk, 0)
    attention = jnp.take(stacked, local_slot * query_rows + local_offset, axis=0, mode="clip")
    out_flat = out_weight.reshape(-1, width_slice)
    block_projection = ring_gather_project(attention, out_flat, req_count, ahead, behind)
    block_of_token = row_of_token // tok_blk
    token_pick = (
        block_of_token[:, None] == jnp.arange(req_count, dtype=jnp.int32)[None, :]
    ).astype(jnp.int32)
    ring_row = jnp.sum(token_pick * ring_slot[None, :], axis=1) * tok_blk + row_of_token % tok_blk
    token_rows = jnp.take(block_projection, ring_row, axis=0, mode="clip")
    projection = lax.psum_scatter(
        token_rows, "kv", scatter_dimension=0, tiled=True
    ).astype(jnp.float32)
    projected = projection.astype(jnp.bfloat16)
    residual = inputs_f32 + projection
    residual_total = lax.psum(jnp.sum(residual * residual, axis=1), "req")
    normed = (
        residual
        * lax.rsqrt(residual_total / width_all + epsilon_norm)[:, None]
        * post_gain.astype(jnp.float32)[None, :]
    ).astype(jnp.bfloat16)
    return (projected, normed, appended)


def solution(mesh):
    in_specs = (
        P("kv", "req"),
        P("req"),
        P("req", "kv", None),
        P("kv", None, "req"),
        P("req"),
        P("req", None, "kv", None),
        P(),
        P(),
        P(),
    )
    out_specs = (P("kv", "req"), P("kv", "req"), P("req", "kv", None))
    return jax.shard_map(
        per_device, mesh=mesh, in_specs=in_specs, out_specs=out_specs, check_vma=False
    )
```

```python
import functools
import math

import jax
import jax.numpy as jnp
import numpy as np
from jax import lax
from jax.experimental import pallas as pl
from jax.experimental.pallas import tpu as pltpu
from jax.sharding import PartitionSpec as P

epsilon_norm = 1e-05
rope_base = 500000.0


def layout(new_lengths, cache_lengths, request_slot, block_tokens):
    blocks, per_block = new_lengths.shape
    request_total = blocks * per_block
    token_total = blocks * block_tokens
    slot_ids = jnp.arange(request_total, dtype=jnp.int32)
    new_flat = new_lengths.reshape(request_total)
    cache_flat = cache_lengths.reshape(request_total)
    chosen = (request_slot[:, None] == slot_ids[None, :]).astype(jnp.int32)
    arrival_len = jnp.sum(chosen * new_flat[None, :], axis=1)
    arrival_start = jnp.cumsum(arrival_len) - arrival_len
    inside = jnp.cumsum(new_lengths, axis=1) - new_lengths
    slot_start = (inside + block_tokens * jnp.arange(blocks, dtype=jnp.int32)[:, None]).reshape(
        request_total
    )
    slot_arrival_start = jnp.sum(chosen * arrival_start[:, None], axis=0)
    positions = jnp.arange(token_total, dtype=jnp.int32)
    slot_of_row = jnp.sum((slot_start[None, :] <= positions[:, None]).astype(jnp.int32), axis=1) - 1
    row_pick = (slot_of_row[:, None] == slot_ids[None, :]).astype(jnp.int32)
    offset_row = positions - jnp.sum(row_pick * slot_start[None, :], axis=1)
    token_of_row = jnp.sum(row_pick * slot_arrival_start[None, :], axis=1) + offset_row
    pos_of_row = jnp.sum(row_pick * cache_flat[None, :], axis=1) + offset_row
    arrival_of_token = (
        jnp.sum((arrival_start[None, :] <= positions[:, None]).astype(jnp.int32), axis=1) - 1
    )
    token_pick = (arrival_of_token[:, None] == slot_ids[None, :]).astype(jnp.int32)
    slot_of_token = jnp.sum(token_pick * request_slot[None, :], axis=1)
    offset_token = positions - jnp.sum(token_pick * arrival_start[None, :], axis=1)
    token_slot_pick = (slot_of_token[:, None] == slot_ids[None, :]).astype(jnp.int32)
    row_of_token = jnp.sum(token_slot_pick * slot_start[None, :], axis=1) + offset_token
    pos_of_token = jnp.sum(token_slot_pick * cache_flat[None, :], axis=1) + offset_token
    return (token_of_row, row_of_token, pos_of_row, pos_of_token, slot_of_row, offset_row)


def rotate(partial_sums, positions, group_size, head_size):
    half_size = head_size // 2
    frequency = jnp.exp(
        -(jnp.arange(half_size, dtype=jnp.float32) * (2.0 / head_size)) * math.log(rope_base)
    )
    angles = positions.astype(jnp.float32)[:, None] * frequency[None, :]
    cosine = jnp.cos(angles)[:, None, None, :]
    sine_part = jnp.sin(angles)[:, None, None, :]
    turned = partial_sums[:, :, : group_size + 1, :]
    first_half = turned[..., :half_size]
    second_half = turned[..., half_size:]
    turned = jnp.concatenate(
        [
            first_half * cosine - second_half * sine_part,
            second_half * cosine + first_half * sine_part,
        ],
        axis=-1,
    )
    return jnp.concatenate([turned, partial_sums[:, :, group_size + 1 :, :]], axis=2)


def attention_kernel(
    group_size, key_block, cached_ref, new_ref, q_ref, key_ref, value_ref, stored_ref, out_ref, keys, values, scores
):
    slot = pl.program_id(0)
    cached_count = cached_ref[slot]
    new_count = new_ref[slot]
    heads, rows_all, head_size = q_ref.shape[1:]
    most_new = key_ref.shape[2]
    slot_length = stored_ref.shape[1]
    chunk = min(256, rows_all)
    chunk_tokens = chunk // group_size
    block_count = (cached_count + key_block - 1) // key_block
    scale = math.log2(math.e) / math.sqrt(head_size)

    def split_heads(index, carry):
        at = pl.ds(pl.multiple_of(index * key_block, key_block), key_block)
        for head in range(heads):
            piece = stored_ref[0, at, head, :]
            keys[head, at, :] = piece[:, :head_size]
            values[head, at, :] = piece[:, head_size:]
        return carry

    lax.fori_loop(0, block_count, split_heads, 0)

    def lane_fold(op, value):
        folded = value[:, :head_size]
        for part in range(1, value.shape[1] // head_size):
            folded = op(folded, value[:, part * head_size : (part + 1) * head_size])
        return folded

    contract_last = (((1,), (1,)), ((), ()))
    for head in range(heads):
        for part in range(rows_all // chunk):

            @pl.when(part * chunk_tokens < new_count)
            def _(head=head, part=part):
                rows = pl.ds(part * chunk, chunk)
                query = q_ref[0, head, rows, :]
                columns = lax.broadcasted_iota(jnp.int32, (chunk, most_new), 1)
                offsets = part * chunk_tokens + (
                    lax.broadcasted_iota(jnp.int32, (chunk, most_new), 0) // group_size
                )
                own = lax.dot_general(
                    query, key_ref[0, head], contract_last, preferred_element_type=jnp.float32
                )
                own = jnp.where((columns <= offsets) & (columns < new_count), own, -jnp.inf)
                places = lax.broadcasted_iota(jnp.int32, (chunk, key_block), 1)

                def fill(index, highest):
                    first = pl.multiple_of(index * key_block, key_block)
                    found = lax.dot_general(
                        query,
                        keys[head, pl.ds(first, key_block), :],
                        contract_last,
                        preferred_element_type=jnp.float32,
                    )
                    found = jnp.where(places < cached_count - first, found, -jnp.inf)
                    scores[:, pl.ds(first, key_block)] = found
                    return jnp.maximum(highest, lane_fold(jnp.maximum, found))

                highest = lax.fori_loop(
                    0, block_count, fill, jnp.full((chunk, head_size), -jnp.inf, jnp.float32)
                )
                top = jnp.maximum(
                    jnp.max(highest, axis=1, keepdims=True), jnp.max(own, axis=1, keepdims=True)
                )
                own_weights = jnp.exp2((own - top) * scale)
                summed = jnp.dot(
                    own_weights.astype(jnp.bfloat16),
                    value_ref[0, head],
                    preferred_element_type=jnp.float32,
                )

                def accumulate(index, pair):
                    first = pl.multiple_of(index * key_block, key_block)
                    weights = jnp.exp2((scores[:, pl.ds(first, key_block)] - top) * scale)
                    added = jnp.dot(
                        weights.astype(jnp.bfloat16),
                        values[head, pl.ds(first, key_block), :],
                        preferred_element_type=jnp.float32,
                    )
                    return (pair[0] + lane_fold(jnp.add, weights), pair[1] + added)

                totals, summed = lax.fori_loop(
                    0,
                    block_count,
                    accumulate,
                    (jnp.zeros((chunk, head_size), jnp.float32), summed),
                )
                total = jnp.sum(totals, axis=1, keepdims=True) + jnp.sum(
                    own_weights, axis=1, keepdims=True
                )
                out_ref[0, head, rows, :] = (summed / total).astype(out_ref.dtype)


def block_attention(queries, new_keys, new_values, stored, cached_counts, new_counts, group_size):
    slots, heads, rows, head_size = queries.shape
    most_new = new_keys.shape[2]
    slot_length = stored.shape[1]
    key_block = min(512, slot_length)
    grid_spec = pltpu.PrefetchScalarGridSpec(
        num_scalar_prefetch=2,
        grid=(slots,),
        in_specs=[
            pl.BlockSpec((1, heads, rows, head_size), lambda s, c, n: (s, 0, 0, 0)),
            pl.BlockSpec((1, heads, most_new, head_size), lambda s, c, n: (s, 0, 0, 0)),
            pl.BlockSpec((1, heads, most_new, head_size), lambda s, c, n: (s, 0, 0, 0)),
            pl.BlockSpec((1, slot_length, heads, 2 * head_size), lambda s, c, n: (s, 0, 0, 0)),
        ],
        out_specs=pl.BlockSpec((1, heads, rows, head_size), lambda s, c, n: (s, 0, 0, 0)),
        scratch_shapes=[
            pltpu.VMEM((heads, slot_length, head_size), jnp.bfloat16),
            pltpu.VMEM((heads, slot_length, head_size), jnp.bfloat16),
            pltpu.VMEM((min(256, rows), slot_length), jnp.float32),
        ],
    )
    return pl.pallas_call(
        functools.partial(attention_kernel, group_size, key_block),
        grid_spec=grid_spec,
        out_shape=jax.ShapeDtypeStruct(queries.shape, jnp.bfloat16),
        compiler_params=pltpu.CompilerParams(vmem_limit_bytes=48 << 20),
    )(cached_counts, new_counts, queries, new_keys, new_values, stored)


def ring_table(count):
    across = 1
    while 4 * across * across <= count:
        across *= 2
    along = count // across
    ring = [place * across for place in range(along)]
    for turn, place in enumerate(reversed(range(along))):
        row = [place * across + step for step in range(1, across)]
        ring += row if turn % 2 == 0 else row[::-1]
    order = np.zeros((count, count), np.int32)
    slot_of = np.zeros((count, count), np.int32)
    for start in range(count):
        for step in range(count):
            order[ring[start], step] = ring[(start + step) % count]
            slot_of[ring[start], ring[(start + step) % count]] = step
    ahead = [(ring[i], ring[(i + 1) % count]) for i in range(count)]
    return order, slot_of, ahead, [(b, a) for a, b in ahead]


def ring_project_scatter(rows, weight, count, ahead, behind):
    block = rows.shape[0] // count
    columns = weight.shape[1]
    parts = 2
    width = columns // parts
    made = {}

    def product(index):
        if index not in made:
            made[index] = jnp.dot(
                rows[index * block : (index + 1) * block],
                weight,
                preferred_element_type=jnp.float32,
            )
        return made[index]

    def piece(index, part):
        return product(index % count)[:, part * width : (part + 1) * width]

    forward = [part % 2 == 0 for part in range(parts)]
    held = [piece(-1 if forward[part] else 1, part) for part in range(parts)]
    for step in range(count - 1):
        held = lax.optimization_barrier(held)
        moved = [
            lax.ppermute(held[part], "req", ahead if forward[part] else behind)
            for part in range(parts)
        ]
        held = [
            moved[part] + piece(-2 - step if forward[part] else 2 + step, part)
            for part in range(parts)
        ]
    return jnp.concatenate(held, axis=1)


def ring_gather_project(own, weight, count, ahead, behind):
    results = [None] * count
    results[0] = jnp.dot(own, weight, preferred_element_type=jnp.float32).astype(jnp.bfloat16)
    half = own.shape[1] // 2
    from_behind = from_ahead = own
    for step in range(1, (count + 1) // 2):
        from_behind = lax.ppermute(from_behind, "req", ahead)
        from_ahead = lax.ppermute(from_ahead, "req", behind)
        for index, arrived in ((count - step, from_behind), (step, from_ahead)):
            results[index] = jnp.dot(
                arrived, weight, preferred_element_type=jnp.float32
            ).astype(jnp.bfloat16)
    if count % 2 == 0:
        last = jnp.concatenate(
            [
                lax.ppermute(from_behind[:, :half], "req", ahead),
                lax.ppermute(from_ahead[:, half:], "req", behind),
            ],
            axis=1,
        )
        results[count // 2] = jnp.dot(
            last, weight, preferred_element_type=jnp.float32
        ).astype(jnp.bfloat16)
    return jnp.concatenate(results, axis=0)


def per_device(
    activations,
    input_gain,
    qkv_weight,
    out_weight,
    post_gain,
    cache_entries,
    new_lengths,
    cache_lengths,
    request_slot,
):
    req_count = lax.axis_size("req")
    kv_count = lax.axis_size("kv")
    token_count = activations.shape[0] * kv_count
    tok_blk = token_count // req_count
    query_rows = tok_blk * 3 // 4
    width_slice = activations.shape[1]
    width_all = width_slice * req_count
    kvh_local = qkv_weight.shape[1]
    head_size = cache_entries.shape[3] // 2
    group_size = qkv_weight.shape[2] // head_size - 2
    per_block = cache_entries.shape[0]
    token_of_row, row_of_token, pos_of_row, pos_of_token, slot_of_row, offset_row = layout(
        new_lengths, cache_lengths, request_slot, tok_blk
    )
    inputs_f32 = activations.astype(jnp.float32)
    square_total = lax.psum(jnp.sum(inputs_f32 * inputs_f32, axis=1), "req")
    normed_in = (
        inputs_f32
        * lax.rsqrt(square_total / width_all + epsilon_norm)[:, None]
        * input_gain.astype(jnp.float32)[None, :]
    ).astype(jnp.bfloat16)
    rows_all = lax.all_gather(normed_in, "kv", axis=0, tiled=True)
    block_id = lax.axis_index("req")
    first_row = block_id * tok_blk
    order, slot_of, ahead, behind = ring_table(req_count)
    ring_order = lax.dynamic_index_in_dim(jnp.asarray(order), block_id, 0, keepdims=False)
    ring_slot = lax.dynamic_index_in_dim(jnp.asarray(slot_of), block_id, 0, keepdims=False)
    ring_pick = (
        ring_order[:, None] == jnp.arange(req_count, dtype=jnp.int32)[None, :]
    ).astype(jnp.int32)
    ring_rows = jnp.sum(
        ring_pick[:, :, None] * token_of_row.reshape(req_count, tok_blk)[None], axis=1
    ).reshape(-1)
    rows_all = jnp.take(rows_all, ring_rows, axis=0, mode="clip")
    weight_flat = qkv_weight.reshape(width_slice, -1)
    qkv_sums = ring_project_scatter(rows_all, weight_flat, req_count, ahead, behind)
    my_positions = lax.dynamic_slice_in_dim(pos_of_row, first_row, tok_blk, 0)
    rotated = rotate(
        qkv_sums.reshape(tok_blk, kvh_local, group_size + 2, head_size),
        my_positions,
        group_size,
        head_size,
    ).astype(jnp.bfloat16)
    appended = rotated[:, :, group_size:, :].reshape(tok_blk, kvh_local, 2 * head_size)
    new_counts = lax.dynamic_index_in_dim(new_lengths, block_id, 0, keepdims=False)
    cached_counts = lax.dynamic_index_in_dim(cache_lengths, block_id, 0, keepdims=False)
    starts = jnp.cumsum(new_counts) - new_counts
    picked = jnp.minimum(
        starts[:, None] + jnp.arange(query_rows, dtype=jnp.int32)[None, :], tok_blk - 1
    ).reshape(-1)
    slot_rows = jnp.take(rotated.reshape(tok_blk, -1), picked, axis=0, mode="clip").reshape(
        per_block, query_rows, kvh_local, group_size + 2, head_size
    )
    queries = jnp.transpose(slot_rows[:, :, :, :group_size], (0, 2, 1, 3, 4)).reshape(
        per_block, kvh_local, query_rows * group_size, head_size
    )
    stacked = block_attention(
        queries,
        jnp.transpose(slot_rows[:, :, :, group_size], (0, 2, 1, 3)),
        jnp.transpose(slot_rows[:, :, :, group_size + 1], (0, 2, 1, 3)),
        cache_entries,
        cached_counts,
        new_counts,
        group_size,
    )
    stacked = jnp.transpose(
        stacked.reshape(per_block, kvh_local, query_rows, -1), (0, 2, 1, 3)
    ).reshape(per_block * query_rows, -1)
    local_slot = lax.dynamic_slice_in_dim(slot_of_row, first_row, tok_blk, 0) - block_id * per_block
    local_offset = lax.dynamic_slice_in_dim(offset_row, first_row, tok_blk, 0)
    attention = jnp.take(stacked, local_slot * query_rows + local_offset, axis=0, mode="clip")
    out_flat = out_weight.reshape(-1, width_slice)
    block_projection = ring_gather_project(attention, out_flat, req_count, ahead, behind)
    block_of_token = row_of_token // tok_blk
    token_pick = (
        block_of_token[:, None] == jnp.arange(req_count, dtype=jnp.int32)[None, :]
    ).astype(jnp.int32)
    ring_row = jnp.sum(token_pick * ring_slot[None, :], axis=1) * tok_blk + row_of_token % tok_blk
    token_rows = jnp.take(block_projection, ring_row, axis=0, mode="clip")
    projection = lax.psum_scatter(
        token_rows, "kv", scatter_dimension=0, tiled=True
    ).astype(jnp.float32)
    projected = projection.astype(jnp.bfloat16)
    residual = inputs_f32 + projection
    residual_total = lax.psum(jnp.sum(residual * residual, axis=1), "req")
    normed = (
        residual
        * lax.rsqrt(residual_total / width_all + epsilon_norm)[:, None]
        * post_gain.astype(jnp.float32)[None, :]
    ).astype(jnp.bfloat16)
    return (projected, normed, appended)


def solution(mesh):
    in_specs = (
        P("kv", "req"),
        P("req"),
        P("req", "kv", None),
        P("kv", None, "req"),
        P("req"),
        P("req", None, "kv", None),
        P(),
        P(),
        P(),
    )
    out_specs = (P("kv", "req"), P("kv", "req"), P("req", "kv", None))
    return jax.shard_map(
        per_device, mesh=mesh, in_specs=in_specs, out_specs=out_specs, check_vma=False
    )
```

```python
import functools
import math

import jax
import jax.numpy as jnp
import numpy as np
from jax import lax
from jax.experimental import pallas as pl
from jax.experimental.pallas import tpu as pltpu
from jax.sharding import PartitionSpec as P

epsilon_norm = 1e-05
rope_base = 500000.0


def layout(new_lengths, cache_lengths, request_slot, block_tokens):
    blocks, per_block = new_lengths.shape
    request_total = blocks * per_block
    token_total = blocks * block_tokens
    slot_ids = jnp.arange(request_total, dtype=jnp.int32)
    new_flat = new_lengths.reshape(request_total)
    cache_flat = cache_lengths.reshape(request_total)
    chosen = (request_slot[:, None] == slot_ids[None, :]).astype(jnp.int32)
    arrival_len = jnp.sum(chosen * new_flat[None, :], axis=1)
    arrival_start = jnp.cumsum(arrival_len) - arrival_len
    inside = jnp.cumsum(new_lengths, axis=1) - new_lengths
    slot_start = (inside + block_tokens * jnp.arange(blocks, dtype=jnp.int32)[:, None]).reshape(
        request_total
    )
    slot_arrival_start = jnp.sum(chosen * arrival_start[:, None], axis=0)
    positions = jnp.arange(token_total, dtype=jnp.int32)
    slot_of_row = jnp.sum((slot_start[None, :] <= positions[:, None]).astype(jnp.int32), axis=1) - 1
    row_pick = (slot_of_row[:, None] == slot_ids[None, :]).astype(jnp.int32)
    offset_row = positions - jnp.sum(row_pick * slot_start[None, :], axis=1)
    token_of_row = jnp.sum(row_pick * slot_arrival_start[None, :], axis=1) + offset_row
    pos_of_row = jnp.sum(row_pick * cache_flat[None, :], axis=1) + offset_row
    arrival_of_token = (
        jnp.sum((arrival_start[None, :] <= positions[:, None]).astype(jnp.int32), axis=1) - 1
    )
    token_pick = (arrival_of_token[:, None] == slot_ids[None, :]).astype(jnp.int32)
    slot_of_token = jnp.sum(token_pick * request_slot[None, :], axis=1)
    offset_token = positions - jnp.sum(token_pick * arrival_start[None, :], axis=1)
    token_slot_pick = (slot_of_token[:, None] == slot_ids[None, :]).astype(jnp.int32)
    row_of_token = jnp.sum(token_slot_pick * slot_start[None, :], axis=1) + offset_token
    pos_of_token = jnp.sum(token_slot_pick * cache_flat[None, :], axis=1) + offset_token
    return (token_of_row, row_of_token, pos_of_row, pos_of_token, slot_of_row, offset_row)


def rotate(partial_sums, positions, group_size, head_size):
    half_size = head_size // 2
    frequency = jnp.exp(
        -(jnp.arange(half_size, dtype=jnp.float32) * (2.0 / head_size)) * math.log(rope_base)
    )
    angles = positions.astype(jnp.float32)[:, None] * frequency[None, :]
    cosine = jnp.cos(angles)[:, None, None, :]
    sine_part = jnp.sin(angles)[:, None, None, :]
    turned = partial_sums[:, :, : group_size + 1, :]
    first_half = turned[..., :half_size]
    second_half = turned[..., half_size:]
    turned = jnp.concatenate(
        [
            first_half * cosine - second_half * sine_part,
            second_half * cosine + first_half * sine_part,
        ],
        axis=-1,
    )
    return jnp.concatenate([turned, partial_sums[:, :, group_size + 1 :, :]], axis=2)


def attention_kernel(
    group_size, key_block, cached_ref, new_ref, q_ref, key_ref, value_ref, stored_ref, out_ref, keys, values, scores
):
    slot = pl.program_id(0)
    cached_count = cached_ref[slot]
    new_count = new_ref[slot]
    heads, rows_all, head_size = q_ref.shape[1:]
    most_new = key_ref.shape[2]
    slot_length = stored_ref.shape[1]
    chunk = min(256, rows_all)
    chunk_tokens = chunk // group_size
    block_count = (cached_count + key_block - 1) // key_block
    scale = math.log2(math.e) / math.sqrt(head_size)

    def split_heads(index, carry):
        at = pl.ds(pl.multiple_of(index * key_block, key_block), key_block)
        for head in range(heads):
            piece = stored_ref[0, at, head, :]
            keys[head, at, :] = piece[:, :head_size]
            values[head, at, :] = piece[:, head_size:]
        return carry

    lax.fori_loop(0, block_count, split_heads, 0)

    def lane_fold(op, value):
        folded = value[:, :head_size]
        for part in range(1, value.shape[1] // head_size):
            folded = op(folded, value[:, part * head_size : (part + 1) * head_size])
        return folded

    contract_last = (((1,), (1,)), ((), ()))
    for head in range(heads):
        for part in range(rows_all // chunk):

            @pl.when(part * chunk_tokens < new_count)
            def _(head=head, part=part):
                rows = pl.ds(part * chunk, chunk)
                query = q_ref[0, head, rows, :]
                columns = lax.broadcasted_iota(jnp.int32, (chunk, most_new), 1)
                offsets = part * chunk_tokens + (
                    lax.broadcasted_iota(jnp.int32, (chunk, most_new), 0) // group_size
                )
                own = lax.dot_general(
                    query, key_ref[0, head], contract_last, preferred_element_type=jnp.float32
                )
                own = jnp.where((columns <= offsets) & (columns < new_count), own, -jnp.inf)
                places = lax.broadcasted_iota(jnp.int32, (chunk, key_block), 1)

                def fill(index, highest):
                    first = pl.multiple_of(index * key_block, key_block)
                    found = lax.dot_general(
                        query,
                        keys[head, pl.ds(first, key_block), :],
                        contract_last,
                        preferred_element_type=jnp.float32,
                    )
                    found = jnp.where(places < cached_count - first, found, -jnp.inf)
                    scores[:, pl.ds(first, key_block)] = found
                    return jnp.maximum(highest, lane_fold(jnp.maximum, found))

                highest = lax.fori_loop(
                    0, block_count, fill, jnp.full((chunk, head_size), -jnp.inf, jnp.float32)
                )
                top = jnp.maximum(
                    jnp.max(highest, axis=1, keepdims=True), jnp.max(own, axis=1, keepdims=True)
                )
                own_weights = jnp.exp2((own - top) * scale)
                summed = jnp.dot(
                    own_weights.astype(jnp.bfloat16),
                    value_ref[0, head],
                    preferred_element_type=jnp.float32,
                )

                def accumulate(index, pair):
                    first = pl.multiple_of(index * key_block, key_block)
                    weights = jnp.exp2((scores[:, pl.ds(first, key_block)] - top) * scale)
                    added = jnp.dot(
                        weights.astype(jnp.bfloat16),
                        values[head, pl.ds(first, key_block), :],
                        preferred_element_type=jnp.float32,
                    )
                    return (pair[0] + lane_fold(jnp.add, weights), pair[1] + added)

                totals, summed = lax.fori_loop(
                    0,
                    block_count,
                    accumulate,
                    (jnp.zeros((chunk, head_size), jnp.float32), summed),
                )
                total = jnp.sum(totals, axis=1, keepdims=True) + jnp.sum(
                    own_weights, axis=1, keepdims=True
                )
                out_ref[0, head, rows, :] = (summed / total).astype(out_ref.dtype)


def block_attention(queries, new_keys, new_values, stored, cached_counts, new_counts, group_size):
    slots, heads, rows, head_size = queries.shape
    most_new = new_keys.shape[2]
    slot_length = stored.shape[1]
    key_block = min(512, slot_length)
    grid_spec = pltpu.PrefetchScalarGridSpec(
        num_scalar_prefetch=2,
        grid=(slots,),
        in_specs=[
            pl.BlockSpec((1, heads, rows, head_size), lambda s, c, n: (s, 0, 0, 0)),
            pl.BlockSpec((1, heads, most_new, head_size), lambda s, c, n: (s, 0, 0, 0)),
            pl.BlockSpec((1, heads, most_new, head_size), lambda s, c, n: (s, 0, 0, 0)),
            pl.BlockSpec((1, slot_length, heads, 2 * head_size), lambda s, c, n: (s, 0, 0, 0)),
        ],
        out_specs=pl.BlockSpec((1, heads, rows, head_size), lambda s, c, n: (s, 0, 0, 0)),
        scratch_shapes=[
            pltpu.VMEM((heads, slot_length, head_size), jnp.bfloat16),
            pltpu.VMEM((heads, slot_length, head_size), jnp.bfloat16),
            pltpu.VMEM((min(256, rows), slot_length), jnp.float32),
        ],
    )
    return pl.pallas_call(
        functools.partial(attention_kernel, group_size, key_block),
        grid_spec=grid_spec,
        out_shape=jax.ShapeDtypeStruct(queries.shape, jnp.bfloat16),
        compiler_params=pltpu.CompilerParams(vmem_limit_bytes=48 << 20),
    )(cached_counts, new_counts, queries, new_keys, new_values, stored)


def ring_table(count):
    across = 1
    while 4 * across * across <= count:
        across *= 2
    along = count // across
    ring = [place * across for place in range(along)]
    for turn, place in enumerate(reversed(range(along))):
        row = [place * across + step for step in range(1, across)]
        ring += row if turn % 2 == 0 else row[::-1]
    order = np.zeros((count, count), np.int32)
    slot_of = np.zeros((count, count), np.int32)
    for start in range(count):
        for step in range(count):
            order[ring[start], step] = ring[(start + step) % count]
            slot_of[ring[start], ring[(start + step) % count]] = step
    ahead = [(ring[i], ring[(i + 1) % count]) for i in range(count)]
    return order, slot_of, ahead, [(b, a) for a, b in ahead]


def ring_project_scatter(rows, weight, count, ahead, behind):
    block = rows.shape[0] // count
    columns = weight.shape[1]
    parts = 2
    width = columns // parts
    made = {}

    def product(index):
        if index not in made:
            made[index] = jnp.dot(
                rows[index * block : (index + 1) * block],
                weight,
                preferred_element_type=jnp.float32,
            )
        return made[index]

    def piece(index, part):
        return product(index % count)[:, part * width : (part + 1) * width]

    forward = [part % 2 == 0 for part in range(parts)]
    held = [piece(-1 if forward[part] else 1, part) for part in range(parts)]
    for step in range(count - 1):
        held = lax.optimization_barrier(held)
        moved = [
            lax.ppermute(held[part], "req", ahead if forward[part] else behind)
            for part in range(parts)
        ]
        held = [
            moved[part] + piece(-2 - step if forward[part] else 2 + step, part)
            for part in range(parts)
        ]
    return jnp.concatenate(held, axis=1)


def ring_gather_project(own, weight, count, ahead, behind):
    results = [None] * count
    results[0] = jnp.dot(own, weight, preferred_element_type=jnp.float32).astype(jnp.bfloat16)
    half = own.shape[1] // 2
    from_behind = from_ahead = own
    for step in range(1, (count + 1) // 2):
        from_behind = lax.ppermute(from_behind, "req", ahead)
        from_ahead = lax.ppermute(from_ahead, "req", behind)
        for index, arrived in ((count - step, from_behind), (step, from_ahead)):
            results[index] = jnp.dot(
                arrived, weight, preferred_element_type=jnp.float32
            ).astype(jnp.bfloat16)
    if count % 2 == 0:
        last = jnp.concatenate(
            [
                lax.ppermute(from_behind[:, :half], "req", ahead),
                lax.ppermute(from_ahead[:, half:], "req", behind),
            ],
            axis=1,
        )
        results[count // 2] = jnp.dot(
            last, weight, preferred_element_type=jnp.float32
        ).astype(jnp.bfloat16)
    return jnp.concatenate(results, axis=0)


def per_device(
    activations,
    input_gain,
    qkv_weight,
    out_weight,
    post_gain,
    cache_entries,
    new_lengths,
    cache_lengths,
    request_slot,
):
    req_count = lax.axis_size("req")
    kv_count = lax.axis_size("kv")
    token_count = activations.shape[0] * kv_count
    tok_blk = token_count // req_count
    query_rows = tok_blk * 3 // 4
    width_slice = activations.shape[1]
    width_all = width_slice * req_count
    kvh_local = qkv_weight.shape[1]
    head_size = cache_entries.shape[3] // 2
    group_size = qkv_weight.shape[2] // head_size - 2
    per_block = cache_entries.shape[0]
    token_of_row, row_of_token, pos_of_row, pos_of_token, slot_of_row, offset_row = layout(
        new_lengths, cache_lengths, request_slot, tok_blk
    )
    inputs_f32 = activations.astype(jnp.float32)
    own_squares = jnp.sum(inputs_f32 * inputs_f32, axis=1)
    own_place = jnp.arange(kv_count, dtype=jnp.int32)[:, None] == lax.axis_index("kv")
    square_total = lax.psum(
        jnp.where(own_place, own_squares[None, :], 0.0).reshape(-1), ("req", "kv")
    )
    rows_all = lax.all_gather(activations, "kv", axis=0, tiled=True)
    rows_all = (
        rows_all.astype(jnp.float32)
        * lax.rsqrt(square_total / width_all + epsilon_norm)[:, None]
        * input_gain.astype(jnp.float32)[None, :]
    ).astype(jnp.bfloat16)
    block_id = lax.axis_index("req")
    first_row = block_id * tok_blk
    order, slot_of, ahead, behind = ring_table(req_count)
    ring_order = lax.dynamic_index_in_dim(jnp.asarray(order), block_id, 0, keepdims=False)
    ring_slot = lax.dynamic_index_in_dim(jnp.asarray(slot_of), block_id, 0, keepdims=False)
    ring_pick = (
        ring_order[:, None] == jnp.arange(req_count, dtype=jnp.int32)[None, :]
    ).astype(jnp.int32)
    ring_rows = jnp.sum(
        ring_pick[:, :, None] * token_of_row.reshape(req_count, tok_blk)[None], axis=1
    ).reshape(-1)
    rows_all = jnp.take(rows_all, ring_rows, axis=0, mode="clip")
    weight_flat = qkv_weight.reshape(width_slice, -1)
    qkv_sums = ring_project_scatter(rows_all, weight_flat, req_count, ahead, behind)
    my_positions = lax.dynamic_slice_in_dim(pos_of_row, first_row, tok_blk, 0)
    rotated = rotate(
        qkv_sums.reshape(tok_blk, kvh_local, group_size + 2, head_size),
        my_positions,
        group_size,
        head_size,
    ).astype(jnp.bfloat16)
    appended = rotated[:, :, group_size:, :].reshape(tok_blk, kvh_local, 2 * head_size)
    new_counts = lax.dynamic_index_in_dim(new_lengths, block_id, 0, keepdims=False)
    cached_counts = lax.dynamic_index_in_dim(cache_lengths, block_id, 0, keepdims=False)
    starts = jnp.cumsum(new_counts) - new_counts
    picked = jnp.minimum(
        starts[:, None] + jnp.arange(query_rows, dtype=jnp.int32)[None, :], tok_blk - 1
    ).reshape(-1)
    slot_rows = jnp.take(rotated.reshape(tok_blk, -1), picked, axis=0, mode="clip").reshape(
        per_block, query_rows, kvh_local, group_size + 2, head_size
    )
    queries = jnp.transpose(slot_rows[:, :, :, :group_size], (0, 2, 1, 3, 4)).reshape(
        per_block, kvh_local, query_rows * group_size, head_size
    )
    stacked = block_attention(
        queries,
        jnp.transpose(slot_rows[:, :, :, group_size], (0, 2, 1, 3)),
        jnp.transpose(slot_rows[:, :, :, group_size + 1], (0, 2, 1, 3)),
        cache_entries,
        cached_counts,
        new_counts,
        group_size,
    )
    stacked = jnp.transpose(
        stacked.reshape(per_block, kvh_local, query_rows, -1), (0, 2, 1, 3)
    ).reshape(per_block * query_rows, -1)
    local_slot = lax.dynamic_slice_in_dim(slot_of_row, first_row, tok_blk, 0) - block_id * per_block
    local_offset = lax.dynamic_slice_in_dim(offset_row, first_row, tok_blk, 0)
    attention = jnp.take(stacked, local_slot * query_rows + local_offset, axis=0, mode="clip")
    out_flat = out_weight.reshape(-1, width_slice)
    block_projection = ring_gather_project(attention, out_flat, req_count, ahead, behind)
    block_of_token = row_of_token // tok_blk
    token_pick = (
        block_of_token[:, None] == jnp.arange(req_count, dtype=jnp.int32)[None, :]
    ).astype(jnp.int32)
    ring_row = jnp.sum(token_pick * ring_slot[None, :], axis=1) * tok_blk + row_of_token % tok_blk
    token_rows = jnp.take(block_projection, ring_row, axis=0, mode="clip")
    projection = lax.psum_scatter(
        token_rows, "kv", scatter_dimension=0, tiled=True
    ).astype(jnp.float32)
    projected = projection.astype(jnp.bfloat16)
    residual = inputs_f32 + projection
    residual_total = lax.psum(jnp.sum(residual * residual, axis=1), "req")
    normed = (
        residual
        * lax.rsqrt(residual_total / width_all + epsilon_norm)[:, None]
        * post_gain.astype(jnp.float32)[None, :]
    ).astype(jnp.bfloat16)
    return (projected, normed, appended)


def solution(mesh):
    in_specs = (
        P("kv", "req"),
        P("req"),
        P("req", "kv", None),
        P("kv", None, "req"),
        P("req"),
        P("req", None, "kv", None),
        P(),
        P(),
        P(),
    )
    out_specs = (P("kv", "req"), P("kv", "req"), P("req", "kv", None))
    return jax.shard_map(
        per_device, mesh=mesh, in_specs=in_specs, out_specs=out_specs, check_vma=False
    )
```
